512 devices in a mesh: lag: 64 (over y, z_hi, x, core), col: 8 (over z_lo).
Axes of the slice: x: 4, y: 4, z: 16 (z_hi: 2, z_lo: 8; z = z_hi * 8 + z_lo), core: 2. Of those that a mesh axis runs over, the one named last changes fastest.
Arguments:
- tap_matrices: bfloat16 [64, 1024, 8192], P('lag', None, 'col'), may hold values from -0.0625 to 0.0625
- density_history: bfloat16 [256, 8192, 128], P('lag', 'col'), may hold values from -6 to 6
- offsets: int32 [64], P('lag'), may hold values from 0 to 3
- column_slots: int32 [8, 128], P('col'), may hold values from 0 to 127, each once within a row
Outputs:
- history_sum: float32 [64, 1024, 3, 128], P('lag', 'col')
The draws below stay inside these ranges and needn't reach their ends.
Inputs may be any that keep to these rules, and one draw needn't show every extreme that they name: Section s reads history slots s * 4 + offsets[s] to s * 4 + offsets[s] + 2. `column_slots`: each row is a permutation of the 128 stored columns.
All inputs are finite; a program needn't handle non-finite values.
Results may differ from the reference program's by a relative error of at most 0.0003.
Values may be sent and summed in bfloat16 or wider, within the bound.
A program may use at most 128 MiB of HBM per device.

```python
import jax
import jax.numpy as jnp
from jax import lax

M = 1024
C = 1024
E = 128
SLOTS = 4
TICKS = 3
SECTIONS = 64
COLS = 8
SRC = 8192
HSLOTS = 256
N_COL = 8


def set_ends(drawn, key, smallest, high):
    longest = drawn.shape.index(max(drawn.shape))
    spots = []
    for shift in (0, 1):
        where = [jax.random.randint(jax.random.fold_in(key, axis), (), 0, length) for axis, length in enumerate(drawn.shape)]
        where[longest] = (where[longest] + shift) % drawn.shape[longest]
        spots.append(tuple(where))
    return drawn.at[spots[0]].set(smallest).at[spots[1]].set(high)


def block_scale(key, dims, cuts, smallest, high):
    factor_of, own = 1.0, jax.random.fold_in(key, 6)
    for position, blocks in cuts:
        heights = jnp.exp(jax.random.uniform(jax.random.fold_in(own, position), (blocks,), jnp.float32, smallest / len(cuts), high / len(cuts)))
        factor_of = factor_of * jnp.repeat(heights, dims[position] // blocks).reshape([-1 if axis == position else 1 for axis in range(len(dims))])
    return factor_of


def scatter_about(own_key, dims, width, bound, cuts=(), kind=jnp.bfloat16):
    entries = width * jax.random.normal(own_key, dims, jnp.float32)
    if cuts:
        entries = entries * block_scale(own_key, dims, cuts, -0.22, 0.18)
    return jnp.clip(entries, -bound, bound).astype(kind)


def setup_inputs(seed: int = 0) -> dict:
    keys = jax.random.split(jax.random.key(seed), 5)
    tap_matrices = scatter_about(keys[0], (SECTIONS, M, SRC), SRC ** -0.5, 0.0625, ((0, 64), (2, 8)))
    density_history = scatter_about(keys[1], (HSLOTS, SRC, E), 1.0, 6.0, ((0, 64), (1, 8)))
    offsets = set_ends(jax.random.randint(keys[2], (SECTIONS,), 0, SLOTS), jax.random.fold_in(keys[2], 1), 0, SLOTS - 1).astype(jnp.int32)
    column_slots = jax.vmap(lambda own: jax.random.permutation(own, E))(jax.random.split(keys[3], COLS)).reshape((COLS, E)).astype(jnp.int32)
    return dict(tap_matrices=tap_matrices, density_history=density_history, offsets=offsets, column_slots=column_slots)


def reorder_group(group_data, group_slots):
    return jnp.take(group_data, group_slots, axis=2)


def reference(tap_matrices, density_history, offsets, column_slots):
    slots_all = density_history.shape[0]
    grouped = density_history.reshape(slots_all, N_COL, C, E)
    ordered = jax.vmap(reorder_group, in_axes=(1, 0), out_axes=1)(grouped, column_slots)
    padded = jnp.concatenate([ordered, jnp.zeros((SLOTS, N_COL, C, E), jnp.bfloat16)], axis=0)

    def advance(running, inputs):
        tap_matrix, offset, section = inputs
        first_slot = (section * SLOTS + offset).astype(jnp.int32)
        densities = lax.dynamic_slice_in_dim(padded, first_slot, TICKS, 0)
        tap_blocks = tap_matrix.reshape(M, N_COL, C)
        partials = jnp.einsum("mgc,tgce->gmte", tap_blocks.astype(jnp.float32), densities.astype(jnp.float32))
        section_sum = jnp.sum(partials, axis=0)
        running = running + section_sum
        return running, running

    start_sum = jnp.zeros((M, TICKS, E), jnp.float32)
    sections_idx = jnp.arange(SECTIONS, dtype=jnp.int32)
    _, history_sum = lax.scan(advance, start_sum, (tap_matrices, offsets, sections_idx))
    return history_sum
```

```python
import functools

import jax
import jax.numpy as jnp
from jax import lax
from jax.experimental import pallas as pl
from jax.experimental.pallas import tpu as pltpu
from jax.sharding import PartitionSpec as P

MESH = pl.DeviceIdType.MESH
NX, NY = 4, 4
TICKS = 3
E = 128
HALVES = 2
HOP = 4
RELAY = 10
D2, D3, D4, D5 = 4, 8, 20, 24


def kernel(zl, off_ref, slots_ref, tap_hbm, dens_hbm, out_ref, tap, win, dmat, prod, rin, lin, gath, pre, tot, yin, exb, zout, zin,
           fin, res, rela, relb, loc, nb_s, nb_r, ca_s, ca_r, cb_s, cb_r, cd_s, cd_r, rs, rr, ls, lr, a_s, a_r, y_s, y_r, z_s, z_r,
           b_s, b_r):
    lag, p = lax.axis_index("lag"), lax.axis_index("col")
    core = lag % 2
    x = (lag // 2) % NX
    zh = (lag // (2 * NX)) % 2
    y = lag // (4 * NX)
    lanes = 2 * NX
    lane = x * 2 + core
    groups = TICKS * HALVES
    rows = prod.shape[2]
    piece = rows // lanes
    part = win.shape[1] // NX
    last = zl - 1

    def at(y_, zh_, x_, core_, p_):
        return (((y_ * 2 + zh_) * NX + x_) * 2 + core_, p_)

    def send(src, dst, ssem, rsem, to):
        return pltpu.make_async_remote_copy(src, dst, ssem, rsem, device_id=to, device_id_type=MESH)

    when = pl.when

    me = (lag, p)
    get_tap = pltpu.make_async_copy(tap_hbm, tap, loc.at[0])
    get_dens = pltpu.make_async_copy(dens_hbm, win.at[pl.ds(0, 4)], loc.at[1])
    get_dens.start()
    get_tap.start()

    cross_src = (x == 0) & (core == 0)
    cross_dst = (x == NX - 1) & (core == 1)
    final = lag == NY * 2 * lanes - 1

    def neighbour():
        return send(dens_hbm.at[pl.ds(0, 2)], win.at[pl.ds(4, 2)], nb_s.at[0], nb_r.at[0], (lag - 1, p))

    @when(jnp.logical_not(cross_src))
    def _():
        neighbour().start()

    def leg_a(j, way):
        k = 2 * j + way
        src = dens_hbm.at[k // NX, pl.ds((k % NX) * part, part)]
        return send(src, rela.at[way], ca_s.at[k], ca_r.at[way], at(y, zh, j, 1, p))

    sends_a = cross_src & (lag > 0)

    @when(sends_a)
    def _():
        for j in range(NX):
            for way in range(2):
                leg_a(j, way).start()

    z = zh * zl + p

    def leg_b(way):
        far = (z + (last if way == 0 else 2 * zl - last)) % (2 * zl)
        return send(rela.at[way], relb.at[way], cb_s.at[way], cb_r.at[way], at(y, far // zl, x, 1, far % zl))

    has_a = (core == 1) & ((y > 0) | (zh == 1))

    @when(has_a)
    def _():
        for way in range(2):
            leg_a(0, way).wait_recv()
            leg_b(way).start()

    def source_zh(way):
        return ((z + (2 * zl - last if way == 0 else last)) % (2 * zl)) // zl

    def has_b(way):
        return (core == 1) & ((y > 0) | (source_zh(way) == 1))

    def leg_d(way):
        to = (z + (1 if way == 0 else 2 * zl - 1)) % (2 * zl)
        y_to = y - (1 - source_zh(way))
        k = 2 * x + way
        dst = win.at[4 + k // NX, pl.ds((k % NX) * part, part)]
        return send(relb.at[way], dst, cd_s.at[way], cd_r.at[k], at(y_to, to // zl, NX - 1, 1, to % zl))

    def relay(mine):
        for way in range(2):

            @when(mine & has_b(way))
            def _(way=way):
                leg_b(way).wait_recv()
                leg_d(way).start()

    relay(x == NX - 1)

    @when(final)
    def _():
        win[pl.ds(4, 2)] = jnp.zeros((2, *win.shape[1:]), win.dtype)

    get_dens.wait()

    @when(jnp.logical_not(cross_dst))
    def _():
        neighbour().wait_recv()

    @when(cross_dst & jnp.logical_not(final))
    def _():
        for k in range(2 * NX):
            dst = win.at[4 + k // NX, pl.ds((k % NX) * part, part)]
            send(relb.at[0], dst, cd_s.at[0], cd_r.at[k], me).wait_recv()

    perm = (lax.broadcasted_iota(jnp.int32, (E, E), 0) == slots_ref[...]).astype(jnp.float32).astype(jnp.bfloat16)
    first = off_ref[0]
    for t in range(TICKS):
        dmat[:, t * E : (t + 1) * E] = jnp.dot(win[first + t], perm, preferred_element_type=jnp.float32).astype(jnp.bfloat16)
    get_tap.wait()
    chunk = rows * HALVES

    def product(d, _):
        block = jnp.dot(tap[pl.ds(pl.multiple_of(d * chunk, chunk), chunk), :], dmat[...], preferred_element_type=jnp.float32)
        for t in range(TICKS):
            for h in range(HALVES):
                prod[d, t * HALVES + h] = block[h * rows : (h + 1) * rows, t * E : (t + 1) * E]
        return 0

    lax.fori_loop(0, zl, product, 0)

    def move(step, hops, sign, buf, ssem, rsem):
        n = step - HOP * hops
        count = jnp.where(hops == 0, last, zl - hops) * groups

        @when((n >= 0) & (n < count))
        def _():
            i = n // groups
            g = n % groups
            d = last - i if sign > 0 else i

            @when(hops > 0)
            def _():
                send(prod.at[d, g], buf.at[d, g], ssem.at[d, g], rsem.at[d, g], me).wait_recv()
                prod[d, g] = prod[d, g] + buf[d, g]

            @when(d != p)
            def _():
                send(prod.at[d, g], buf.at[d, g], ssem.at[d, g], rsem.at[d, g], (lag, p + sign)).start()

    def peers(body):
        for j in range(lanes):

            @when(j != lane)
            def _(j=j):
                body(j)

    def mine(j):
        return pl.ds(j * piece, piece)

    def lane_at(j):
        return at(y, zh, j // 2, j % 2, p)

    def out_copy(g, j):
        return send(prod.at[p, g, mine(j)], gath.at[g, lane], a_s.at[g, j], a_r.at[g, lane], lane_at(j))

    def back_copy(g, j):
        return send(fin.at[g, j], res.at[g, mine(lane)], b_s.at[g, j], b_r.at[g, lane], lane_at(j))

    def y_copy(g, j):
        return send(tot.at[g], yin.at[g, y], y_s.at[g, j], y_r.at[g, y], at(j, zh, x, core, p))

    def z_copy(g):
        return send(zout.at[g], zin.at[g], z_s.at[g], z_r.at[g], at(y, 1 - zh, x, core, p))

    def stage1(g):
        gath[g, lane] = prod[p, g, pl.ds(pl.multiple_of(lane * piece, piece), piece)]
        peers(lambda j: out_copy(g, j).start())

    def stage2(g):
        peers(lambda j: send(prod.at[p, g, mine(j)], gath.at[g, j], a_s.at[g, j], a_r.at[g, j], me).wait_recv())
        c = gath[g, 0]
        pre[g, 0] = c
        for j in range(1, lanes):
            c = c + gath[g, j]
            pre[g, j] = c
        tot[g] = c
        for j in range(1, NY):

            @when(j > y)
            def _(j=j):
                y_copy(g, j).start()

    def stage3(g):
        exb[g] = jnp.zeros(exb.shape[1:], exb.dtype)
        for j in range(NY - 1):

            @when(j < y)
            def _(j=j):
                send(tot.at[g], yin.at[g, j], y_s.at[g, j], y_r.at[g, j], me).wait_recv()
                exb[g] = exb[g] + yin[g, j]

        zout[g] = exb[g] + jnp.where(zh == 0, tot[g], 0.0)
        z_copy(g).start()

    def stage4(g):
        z_copy(g).wait_recv()
        e = exb[g] + zin[g]
        for j in range(lanes):
            fin[g, j] = pre[g, j] + e
        res[g, pl.ds(pl.multiple_of(lane * piece, piece), piece)] = fin[g, lane]
        peers(lambda j: back_copy(g, j).start())

    def stage5(g):
        peers(lambda j: send(fin.at[g, j], res.at[g, mine(j)], b_s.at[g, j], b_r.at[g, j], me).wait_recv())
        out_ref[g // HALVES, pl.ds(pl.multiple_of((g % HALVES) * rows, rows), rows)] = res[g]

    def ready(q):
        right = jnp.where(q > 0, HOP * q + (last - q) * groups, 0)
        left = jnp.where(q < last, HOP * (last - q) + q * groups, 0)
        return jnp.maximum(right, left)

    base = ready(p)
    longest = max(max(HOP * q + (last - q) * groups if q else 0, HOP * (last - q) + q * groups if q < last else 0) for q in range(zl))

    def step(s, _):
        move(s, p, 1, rin, rs, rr)
        move(s, last - p, -1, lin, ls, lr)

        @when(s == RELAY)
        def _():
            relay(x < NX - 1)

        for delay, stage in ((0, stage1), (D2, stage2), (D3, stage3), (D4, stage4), (D5, stage5)):
            g = s - base - delay

            @when((g >= 0) & (g < groups))
            def _(g=g, stage=stage):
                stage(g)

        return 0

    lax.fori_loop(0, longest + groups + D5, step, 0)

    @when(jnp.logical_not(cross_src))
    def _():
        neighbour().wait_send()

    @when(sends_a)
    def _():
        for j in range(NX):
            for way in range(2):
                leg_a(j, way).wait_send()

    @when(has_a)
    def _():
        for way in range(2):
            leg_b(way).wait_send()

    for way in range(2):

        @when(has_b(way))
        def _(way=way):
            leg_d(way).wait_send()

    def drain(d, _):
        def one(g, _):
            @when(d > p)
            def _():
                send(prod.at[d, g], rin.at[d, g], rs.at[d, g], rr.at[d, g], me).wait_send()

            @when(d < p)
            def _():
                send(prod.at[d, g], lin.at[d, g], ls.at[d, g], lr.at[d, g], me).wait_send()

            return 0

        return lax.fori_loop(0, groups, one, 0)

    lax.fori_loop(0, zl, drain, 0)

    def drain_scan(g, _):
        peers(lambda j: out_copy(g, j).wait_send())
        peers(lambda j: back_copy(g, j).wait_send())
        for j in range(1, NY):

            @when(j > y)
            def _(j=j):
                y_copy(g, j).wait_send()

        z_copy(g).wait_send()
        return 0

    lax.fori_loop(0, groups, drain_scan, 0)


def local(zl, tap_matrices, density_history, offsets, column_slots):
    m, c = tap_matrices.shape[1:]
    chunk = m // zl
    groups, rows, lanes = TICKS * HALVES, chunk // HALVES, 2 * NX
    piece, part = rows // lanes, c // NX
    f32, bf16 = jnp.float32, jnp.bfloat16
    vmem, dma = pltpu.VMEM, pltpu.SemaphoreType.DMA
    out = pl.pallas_call(
        functools.partial(kernel, zl),
        out_shape=jax.ShapeDtypeStruct((TICKS, chunk, E), f32),
        in_specs=[
            pl.BlockSpec(memory_space=pltpu.SMEM),
            pl.BlockSpec(memory_space=pltpu.VMEM),
            pl.BlockSpec(memory_space=pl.ANY),
            pl.BlockSpec(memory_space=pl.ANY),
        ],
        out_specs=pl.BlockSpec(memory_space=pltpu.VMEM),
        scratch_shapes=[
            vmem((m, c), bf16),
            vmem((6, c, E), bf16),
            vmem((c, TICKS * E), bf16),
            vmem((zl, groups, rows, E), f32),
            vmem((zl, groups, rows, E), f32),
            vmem((zl, groups, rows, E), f32),
            vmem((groups, lanes, piece, E), f32),
            vmem((groups, lanes, piece, E), f32),
            vmem((groups, piece, E), f32),
            vmem((groups, NY, piece, E), f32),
            vmem((groups, piece, E), f32),
            vmem((groups, piece, E), f32),
            vmem((groups, piece, E), f32),
            vmem((groups, lanes, piece, E), f32),
            vmem((groups, rows, E), f32),
            vmem((2, part, E), bf16),
            vmem((2, part, E), bf16),
            dma((2,)),
            dma((1,)), dma((1,)),
            dma((2 * NX,)), dma((2,)),
            dma((2,)), dma((2,)),
            dma((2,)), dma((2 * NX,)),
            dma((zl, groups)), dma((zl, groups)),
            dma((zl, groups)), dma((zl, groups)),
            dma((groups, lanes)), dma((groups, lanes)),
            dma((groups, NY)), dma((groups, NY)),
            dma((groups,)), dma((groups,)),
            dma((groups, lanes)), dma((groups, lanes)),
        ],
        compiler_params=pltpu.CompilerParams(has_side_effects=True, vmem_limit_bytes=40 << 20),
    )(offsets, column_slots, tap_matrices.reshape(m, c), density_history)
    return out.transpose(1, 0, 2)[None]


def solution(mesh):
    return jax.shard_map(
        functools.partial(local, mesh.shape["col"]),
        mesh=mesh,
        in_specs=(P("lag", None, "col"), P("lag", "col", None), P("lag"), P("col", None)),
        out_specs=P("lag", "col", None, None),
        check_vma=False,
    )
```

```python
import functools

import jax
import jax.numpy as jnp
from jax import lax
from jax.experimental import pallas as pl
from jax.experimental.pallas import tpu as pltpu
from jax.sharding import PartitionSpec as P

MESH = pl.DeviceIdType.MESH
NX, NY = 4, 4
TICKS = 3
E = 128
HALVES = 2
HOP = 6
D2, D3, D4, D5 = 8, 16, 32, 40


def kernel(zl, off_ref, slots_hbm, tap_hbm, dens_hbm, out_ref, slots_ref, tap, win, dmat, prod, rin, lin, gath, pre, tot, yin, exb, zout, zin,
           fin, res, rela, loc, nb_s, nb_r, ca_s, ca_r, cb_s, cb_r, hello, rs, rr, ls, lr, a_s, a_r, y_s, y_r, z_s, z_r,
           b_s, b_r):
    lag, p = lax.axis_index("lag"), lax.axis_index("col")
    core = lag % 2
    x = (lag // 2) % NX
    zh = (lag // (2 * NX)) % 2
    y = lag // (4 * NX)
    lanes = 2 * NX
    lane = x * 2 + core
    groups = TICKS * HALVES
    rows = prod.shape[2]
    piece = rows // lanes
    part = win.shape[1] // (NX // 2)
    last = zl - 1

    def at(y_, zh_, x_, core_, p_):
        return (((y_ * 2 + zh_) * NX + x_) * 2 + core_, p_)

    def send(src, dst, ssem, rsem, to):
        return pltpu.make_async_remote_copy(src, dst, ssem, rsem, device_id=to, device_id_type=MESH)

    when = pl.when

    me = (lag, p)
    get_tap = pltpu.make_async_copy(tap_hbm, tap, loc.at[0])
    get_dens = pltpu.make_async_copy(dens_hbm, win.at[pl.ds(0, 4)], loc.at[1])
    get_slots = pltpu.make_async_copy(slots_hbm, slots_ref, loc.at[2])
    get_dens.start()
    get_tap.start()
    get_slots.start()
    z = zh * zl + p

    def round_z(q):
        q = (q + 2 * zl) % (2 * zl)
        return q // zl, q % zl

    cross_src = (x == 0) & (core == 0)
    cross_dst = (x == NX - 1) & (core == 1)
    final = lag == NY * 2 * lanes - 1
    sends_a = cross_src & (lag > 0)
    has_a = (core == 1) & ((y > 0) | (zh == 1))

    def middle(zh_):
        return (core == 1) & ((y > 0) | (zh_ == 1))

    barrier = pltpu.get_barrier_semaphore()

    def greet(to):
        pl.semaphore_signal(barrier, inc=1, device_id=to, device_id_type=MESH)

    for j in range(lanes):

        @when(j != lane)
        def _(j=j):
            greet(at(y, zh, j // 2, j % 2, p))

    @when(p > 0)
    def _():
        greet((lag, p - 1))

    @when(p < last)
    def _():
        greet((lag, p + 1))

    for j in range(NY - 1):

        @when(j < y)
        def _(j=j):
            greet(at(j, zh, x, core, p))

    ahead, behind = round_z(z + zl // 2), round_z(z - zl // 2)
    greet(at(y, ahead[0], x, core, ahead[1]))
    greet(at(y, behind[0], x, core, behind[1]))

    @when(cross_dst & jnp.logical_not(final))
    def _():
        for j in range(NX):
            greet(at(y + zh, ahead[0], j, 1, ahead[1]))

    one = lambda c: c.astype(jnp.int32)
    many = lanes - 1 + one(p > 0) + one(p < last) + NY - 1 - y + 2 + one(middle(ahead[0]))
    pl.semaphore_wait(barrier, many)
    pl.semaphore_signal(hello, inc=1, device_id=at(y, ahead[0], x, core, ahead[1]), device_id_type=MESH)

    def neighbour():
        return send(dens_hbm.at[pl.ds(0, 2)], win.at[pl.ds(4, 2)], nb_s.at[0], nb_r.at[0], (lag - 1, p))

    @when(jnp.logical_not(cross_src))
    def _():
        neighbour().start()

    def part_of(ref, j, first):
        return ref.at[first + j // (NX // 2), pl.ds((j % (NX // 2)) * part, part)]

    def leg_a(j):
        return send(part_of(dens_hbm, j, 0), rela, ca_s.at[j], ca_r.at[0], at(y, zh, j, 1, p))

    def leg_b():
        return send(rela, part_of(win, x, 4), cb_s.at[0], cb_r.at[x], at(y - (1 - zh), 1 - zh, NX - 1, 1, p))

    @when(sends_a)
    def _():
        for j in range(NX):
            leg_a(j).start()

    pl.semaphore_wait(hello, 1)

    @when(has_a)
    def _():
        leg_a(0).wait_recv()
        leg_b().start()

    @when(final)
    def _():
        win[pl.ds(4, 2)] = jnp.zeros((2, *win.shape[1:]), win.dtype)

    get_dens.wait()

    @when(jnp.logical_not(cross_dst))
    def _():
        neighbour().wait_recv()

    @when(cross_dst & jnp.logical_not(final))
    def _():
        for j in range(NX):
            send(rela, part_of(win, j, 4), cb_s.at[0], cb_r.at[j], me).wait_recv()

    get_slots.wait()
    perm = (lax.broadcasted_iota(jnp.int32, (E, E), 0) == slots_ref[...]).astype(jnp.float32).astype(jnp.bfloat16)
    first = off_ref[0]
    for t in range(TICKS):
        dmat[:, t * E : (t + 1) * E] = jnp.dot(win[first + t], perm, preferred_element_type=jnp.float32).astype(jnp.bfloat16)
    get_tap.wait()
    chunk = rows * HALVES

    def product(k):
        d = jnp.where(k % 2 == 0, last - k // 2, k // 2)
        block = jnp.dot(tap[pl.ds(pl.multiple_of(d * chunk, chunk), chunk), :], dmat[...], preferred_element_type=jnp.float32)
        for t in range(TICKS):
            for h in range(HALVES):
                prod[d, t * HALVES + h] = block[h * rows : (h + 1) * rows, t * E : (t + 1) * E]

    def first_two(k, _):
        product(k)
        return 0

    lax.fori_loop(0, 2, first_two, 0)

    def move(step, hops, sign, buf, ssem, rsem):
        n = step - HOP * hops
        count = jnp.where(hops == 0, last, zl - hops) * groups

        @when((n >= 0) & (n < count))
        def _():
            i = n // groups
            g = n % groups
            d = last - i if sign > 0 else i

            @when(hops > 0)
            def _():
                send(prod.at[d, g], buf.at[d, g], ssem.at[d, g], rsem.at[d, g], me).wait_recv()
                prod[d, g] = prod[d, g] + buf[d, g]

            @when(d != p)
            def _():
                send(prod.at[d, g], buf.at[d, g], ssem.at[d, g], rsem.at[d, g], (lag, p + sign)).start()

    def peers(body):
        for j in range(lanes):

            @when(j != lane)
            def _(j=j):
                body(j)

    def mine(j):
        return pl.ds(j * piece, piece)

    def lane_at(j):
        return at(y, zh, j // 2, j % 2, p)

    def out_copy(g, j):
        return send(prod.at[p, g, mine(j)], gath.at[g, lane], a_s.at[g, j], a_r.at[g, lane], lane_at(j))

    def back_copy(g, j):
        return send(fin.at[g, j], res.at[g, mine(lane)], b_s.at[g, j], b_r.at[g, lane], lane_at(j))

    def y_copy(g, j):
        return send(tot.at[g], yin.at[g, y], y_s.at[g, j], y_r.at[g, y], at(j, zh, x, core, p))

    def z_copy(g):
        return send(zout.at[g], zin.at[g], z_s.at[g], z_r.at[g], at(y, 1 - zh, x, core, p))

    def stage1(g):
        gath[g, lane] = prod[p, g, pl.ds(pl.multiple_of(lane * piece, piece), piece)]
        peers(lambda j: out_copy(g, j).start())

    def stage2(g):
        peers(lambda j: send(prod.at[p, g, mine(j)], gath.at[g, j], a_s.at[g, j], a_r.at[g, j], me).wait_recv())
        c = gath[g, 0]
        pre[g, 0] = c
        for j in range(1, lanes):
            c = c + gath[g, j]
            pre[g, j] = c
        tot[g] = c
        for j in range(1, NY):

            @when(j > y)
            def _(j=j):
                y_copy(g, j).start()

    def stage3(g):
        exb[g] = jnp.zeros(exb.shape[1:], exb.dtype)
        for j in range(NY - 1):

            @when(j < y)
            def _(j=j):
                send(tot.at[g], yin.at[g, j], y_s.at[g, j], y_r.at[g, j], me).wait_recv()
                exb[g] = exb[g] + yin[g, j]

        zout[g] = exb[g] + jnp.where(zh == 0, tot[g], 0.0)
        z_copy(g).start()

    def stage4(g):
        z_copy(g).wait_recv()
        e = exb[g] + zin[g]
        for j in range(lanes):
            fin[g, j] = pre[g, j] + e
        res[g, pl.ds(pl.multiple_of(lane * piece, piece), piece)] = fin[g, lane]
        peers(lambda j: back_copy(g, j).start())

    def stage5(g):
        peers(lambda j: send(fin.at[g, j], res.at[g, mine(j)], b_s.at[g, j], b_r.at[g, j], me).wait_recv())
        out_ref[g // HALVES, pl.ds(pl.multiple_of((g % HALVES) * rows, rows), rows)] = res[g]

    def ready(q):
        right = jnp.where(q > 0, HOP * q + (last - q) * groups, 0)
        left = jnp.where(q < last, HOP * (last - q) + q * groups, 0)
        return jnp.maximum(right, left)

    base = ready(p)
    longest = max(max(HOP * q + (last - q) * groups if q else 0, HOP * (last - q) + q * groups if q < last else 0) for q in range(zl))

    def step(s, _):
        move(s, p, 1, rin, rs, rr)
        move(s, last - p, -1, lin, ls, lr)

        @when(s < zl - 2)
        def _():
            product(s + 2)

        for delay, stage in ((0, stage1), (D2, stage2), (D3, stage3), (D4, stage4), (D5, stage5)):
            g = s - base - delay

            @when((g >= 0) & (g < groups))
            def _(g=g, stage=stage):
                stage(g)

        return 0

    lax.fori_loop(0, longest + groups + D5, step, 0)

    @when(jnp.logical_not(cross_src))
    def _():
        neighbour().wait_send()

    @when(sends_a)
    def _():
        for j in range(NX):
            leg_a(j).wait_send()

    @when(has_a)
    def _():
        leg_b().wait_send()

    def drain(d, _):
        def one(g, _):
            @when(d > p)
            def _():
                send(prod.at[d, g], rin.at[d, g], rs.at[d, g], rr.at[d, g], me).wait_send()

            @when(d < p)
            def _():
                send(prod.at[d, g], lin.at[d, g], ls.at[d, g], lr.at[d, g], me).wait_send()

            return 0

        return lax.fori_loop(0, groups, one, 0)

    lax.fori_loop(0, zl, drain, 0)

    def drain_scan(g, _):
        peers(lambda j: out_copy(g, j).wait_send())
        peers(lambda j: back_copy(g, j).wait_send())
        for j in range(1, NY):

            @when(j > y)
            def _(j=j):
                y_copy(g, j).wait_send()

        z_copy(g).wait_send()
        return 0

    lax.fori_loop(0, groups, drain_scan, 0)


def local(zl, tap_matrices, density_history, offsets, column_slots):
    m, c = tap_matrices.shape[1:]
    chunk = m // zl
    groups, rows, lanes = TICKS * HALVES, chunk // HALVES, 2 * NX
    piece, part = rows // lanes, c // (NX // 2)
    f32, bf16 = jnp.float32, jnp.bfloat16
    vmem, dma = pltpu.VMEM, pltpu.SemaphoreType.DMA
    out = pl.pallas_call(
        functools.partial(kernel, zl),
        out_shape=jax.ShapeDtypeStruct((TICKS, chunk, E), f32),
        in_specs=[
            pl.BlockSpec(memory_space=pltpu.SMEM),
            pl.BlockSpec(memory_space=pl.ANY),
            pl.BlockSpec(memory_space=pl.ANY),
            pl.BlockSpec(memory_space=pl.ANY),
        ],
        out_specs=pl.BlockSpec(memory_space=pltpu.VMEM),
        scratch_shapes=[
            vmem((1, E), jnp.int32),
            vmem((m, c), bf16),
            vmem((6, c, E), bf16),
            vmem((c, TICKS * E), bf16),
            vmem((zl, groups, rows, E), f32),
            vmem((zl, groups, rows, E), f32),
            vmem((zl, groups, rows, E), f32),
            vmem((groups, lanes, piece, E), f32),
            vmem((groups, lanes, piece, E), f32),
            vmem((groups, piece, E), f32),
            vmem((groups, NY, piece, E), f32),
            vmem((groups, piece, E), f32),
            vmem((groups, piece, E), f32),
            vmem((groups, piece, E), f32),
            vmem((groups, lanes, piece, E), f32),
            vmem((groups, rows, E), f32),
            vmem((part, E), bf16),
            dma((3,)),
            dma((1,)), dma((1,)),
            dma((NX,)), dma((1,)),
            dma((1,)), dma((NX,)),
            pltpu.SemaphoreType.REGULAR,
            dma((zl, groups)), dma((zl, groups)),
            dma((zl, groups)), dma((zl, groups)),
            dma((groups, lanes)), dma((groups, lanes)),
            dma((groups, NY)), dma((groups, NY)),
            dma((groups,)), dma((groups,)),
            dma((groups, lanes)), dma((groups, lanes)),
        ],
        compiler_params=pltpu.CompilerParams(collective_id=0, has_side_effects=True, vmem_limit_bytes=62 << 20),
    )(offsets, column_slots, tap_matrices.reshape(m, c), density_history)
    return out.transpose(1, 0, 2)[None]


def solution(mesh):
    return jax.shard_map(
        functools.partial(local, mesh.shape["col"]),
        mesh=mesh,
        in_specs=(P("lag", None, "col"), P("lag", "col", None), P("lag"), P("col", None)),
        out_specs=P("lag", "col", None, None),
        check_vma=False,
    )
```

```python
import functools

import jax
import jax.numpy as jnp
from jax import lax
from jax.experimental import pallas as pl
from jax.experimental.pallas import tpu as pltpu
from jax.sharding import PartitionSpec as P

MESH = pl.DeviceIdType.MESH
NX, NY = 4, 4
TICKS = 3
E = 128
HALVES = 2
HOP = 6
D2, D3, D4, D5 = 7, 14, 29, 36


def kernel(zl, off_ref, slots_hbm, tap_hbm, dens_hbm, out_ref, slots_ref, tap, win, dmat, prod, rin, lin, gath, pre, tot, yin, exb, zout, zin,
           fin, res, rela, loc, nb_s, nb_r, ca_s, ca_r, cb_s, cb_r, hello, rs, rr, ls, lr, a_s, a_r, y_s, y_r, z_s, z_r,
           b_s, b_r):
    lag, p = lax.axis_index("lag"), lax.axis_index("col")
    core = lag % 2
    x = (lag // 2) % NX
    zh = (lag // (2 * NX)) % 2
    y = lag // (4 * NX)
    lanes = 2 * NX
    lane = x * 2 + core
    groups = TICKS * HALVES
    rows = prod.shape[2]
    piece = rows // lanes
    part = win.shape[1] // (NX // 2)
    last = zl - 1

    def at(y_, zh_, x_, core_, p_):
        return (((y_ * 2 + zh_) * NX + x_) * 2 + core_, p_)

    def send(src, dst, ssem, rsem, to):
        return pltpu.make_async_remote_copy(src, dst, ssem, rsem, device_id=to, device_id_type=MESH)

    when = pl.when

    me = (lag, p)
    get_tap = pltpu.make_async_copy(tap_hbm, tap, loc.at[0])
    get_dens = pltpu.make_async_copy(dens_hbm, win.at[pl.ds(0, 4)], loc.at[1])
    get_slots = pltpu.make_async_copy(slots_hbm, slots_ref, loc.at[2])
    get_dens.start()
    get_tap.start()
    get_slots.start()
    z = zh * zl + p

    def round_z(q):
        q = (q + 2 * zl) % (2 * zl)
        return q // zl, q % zl

    cross_src = (x == 0) & (core == 0)
    cross_dst = (x == NX - 1) & (core == 1)
    final = lag == NY * 2 * lanes - 1
    sends_a = cross_src & (lag > 0)
    has_a = (core == 1) & ((y > 0) | (zh == 1))

    barrier = pltpu.get_barrier_semaphore()

    def greet(to):
        pl.semaphore_signal(barrier, inc=1, device_id=to, device_id_type=MESH)

    def loop(count, body):
        def one_more(j, _):
            body(j)
            return 0

        lax.fori_loop(0, count, one_more, 0)

    def others(body):
        loop(lanes - 1, lambda j: body((lane + 1 + j) % lanes))

    others(lambda j: greet(at(y, zh, j // 2, j % 2, p)))

    @when(p > 0)
    def _():
        greet((lag, p - 1))

    @when(p < last)
    def _():
        greet((lag, p + 1))

    loop(y, lambda j: greet(at(j, zh, x, core, p)))

    eighth, quarter = zl // 4, zl // 2

    def along(dz):
        zh_, p_ = round_z(z + dz)
        return at(y, zh_, x, core, p_)

    greet(along(eighth))
    greet(along(-eighth))

    @when(cross_dst & jnp.logical_not(final))
    def _():
        zh_, p_ = round_z(z - eighth)
        for j in range(NX):
            greet(at(y + zh, zh_, j, 1, p_))

    one = lambda c: c.astype(jnp.int32)
    far = round_z(z + eighth)[0]
    many = lanes - 1 + one(p > 0) + one(p < last) + NY - 1 - y + 2 + one((core == 1) & ((y > 0) | (far == 0)))
    pl.semaphore_wait(barrier, many)
    for dz in (eighth, -eighth):
        pl.semaphore_signal(hello.at[0], inc=1, device_id=along(dz), device_id_type=MESH)

    def vouch():
        pl.semaphore_wait(hello.at[0], 2)
        pl.semaphore_signal(hello.at[1], inc=1, device_id=along(-quarter), device_id_type=MESH)

    def vouched():
        pl.semaphore_wait(hello.at[1], 1)

    def neighbour():
        return send(dens_hbm.at[pl.ds(0, 2)], win.at[pl.ds(4, 2)], nb_s.at[0], nb_r.at[0], (lag - 1, p))

    @when(jnp.logical_not(cross_src))
    def _():
        neighbour().start()

    def part_of(ref, j, first):
        return ref.at[first + j // (NX // 2), pl.ds((j % (NX // 2)) * part, part)]

    def leg_a(j):
        return send(part_of(dens_hbm, j, 0), rela, ca_s.at[j], ca_r.at[0], at(y, zh, j, 1, p))

    def leg_b():
        return send(rela, part_of(win, x, 4), cb_s.at[0], cb_r.at[x], at(y - (1 - zh), 1 - zh, NX - 1, 1, p))

    @when(sends_a)
    def _():
        for j in range(NX):
            leg_a(j).start()

    @when(core == 1)
    def _():
        vouch()
        vouched()

    @when(has_a)
    def _():
        leg_a(0).wait_recv()
        leg_b().start()

    @when(final)
    def _():
        win[pl.ds(4, 2)] = jnp.zeros((2, *win.shape[1:]), win.dtype)

    get_dens.wait()

    @when(jnp.logical_not(cross_dst))
    def _():
        neighbour().wait_recv()

    @when(cross_dst & jnp.logical_not(final))
    def _():
        for j in range(NX):
            send(rela, part_of(win, j, 4), cb_s.at[0], cb_r.at[j], me).wait_recv()

    get_slots.wait()
    perm = (lax.broadcasted_iota(jnp.int32, (E, E), 0) == slots_ref[...]).astype(jnp.float32).astype(jnp.bfloat16)
    first = off_ref[0]
    for t in range(TICKS):
        dmat[:, t * E : (t + 1) * E] = jnp.dot(win[first + t], perm, preferred_element_type=jnp.float32).astype(jnp.bfloat16)
    get_tap.wait()
    chunk = rows * HALVES

    def product(k):
        d = jnp.where(k % 2 == 0, last - k // 2, k // 2)
        block = jnp.dot(tap[pl.ds(pl.multiple_of(d * chunk, chunk), chunk), :], dmat[...], preferred_element_type=jnp.float32)
        for t in range(TICKS):
            for h in range(HALVES):
                prod[d, t * HALVES + h] = block[h * rows : (h + 1) * rows, t * E : (t + 1) * E]

    @when(core == 0)
    def _():
        vouch()

    def move(step, hops, sign, buf, ssem, rsem):
        def copy(d, g, to):
            return send(prod.at[d, g], buf.at[d, g], ssem.at[d], rsem.at[d, g], to)

        @when((hops == 0) & (step < last))
        def _():
            d = last - step if sign > 0 else step
            loop(groups, lambda g: copy(d, g, (lag, p + sign)).start())

        n = step - HOP * hops

        @when((hops > 0) & (n >= 0) & (n < (zl - hops) * groups))
        def _():
            i = n // groups
            g = n % groups
            d = last - i if sign > 0 else i
            copy(d, g, me).wait_recv()
            prod[d, g] = prod[d, g] + buf[d, g]

            @when(d != p)
            def _():
                copy(d, g, (lag, p + sign)).start()

    def mine(j):
        return pl.ds(pl.multiple_of(j * piece, piece), piece)

    def lane_at(j):
        return at(y, zh, j // 2, j % 2, p)

    def out_copy(g, j):
        return send(prod.at[p, g, mine(j)], gath.at[g, lane], a_s.at[g], a_r.at[g], lane_at(j))

    def back_copy(g, j):
        return send(fin.at[g, j], res.at[g, mine(lane)], b_s.at[g], b_r.at[g], lane_at(j))

    def y_copy(g, j):
        return send(tot.at[g], yin.at[g, y], y_s.at[g], y_r.at[g], at(j, zh, x, core, p))

    def z_copy(g):
        return send(zout.at[g], zin.at[g], z_s.at[g], z_r.at[g], at(y, 1 - zh, x, core, p))

    def all_of(g, sems, rsems, count):
        some = gath.at[g, pl.ds(0, count)]
        return send(some, some, sems.at[g], rsems.at[g], me)

    def stage1(g):
        gath[g, lane] = prod[p, g, mine(lane)]
        others(lambda j: out_copy(g, j).start())

    def stage2(g):
        all_of(g, a_s, a_r, lanes - 1).wait_recv()
        c = gath[g, 0]
        pre[g, 0] = c
        for j in range(1, lanes):
            c = c + gath[g, j]
            pre[g, j] = c
        tot[g] = c
        loop(NY - 1 - y, lambda j: y_copy(g, y + 1 + j).start())

    def stage3(g):
        exb[g] = jnp.zeros(exb.shape[1:], exb.dtype)
        for q in range(1, NY):

            @when(y == q)
            def _(q=q):
                all_of(g, y_s, y_r, q).wait_recv()

        def add(j):
            exb[g] = exb[g] + yin[g, j]

        loop(y, add)

        @when((core == 0) & (g == 0))
        def _():
            vouched()

        zout[g] = exb[g] + jnp.where(zh == 0, tot[g], 0.0)
        z_copy(g).start()

    def stage4(g):
        z_copy(g).wait_recv()
        e = exb[g] + zin[g]
        for j in range(lanes):
            fin[g, j] = pre[g, j] + e
        res[g, mine(lane)] = fin[g, lane]
        others(lambda j: back_copy(g, j).start())

    def stage5(g):
        all_of(g, b_s, b_r, lanes - 1).wait_recv()
        out_ref[g // HALVES, pl.ds(pl.multiple_of((g % HALVES) * rows, rows), rows)] = res[g]

    def ready(q):
        right = jnp.where(q > 0, HOP * q + (last - q) * groups, 0)
        left = jnp.where(q < last, HOP * (last - q) + q * groups, 0)
        return jnp.maximum(right, left)

    base = ready(p)
    longest = max(max(HOP * q + (last - q) * groups if q else 0, HOP * (last - q) + q * groups if q < last else 0) for q in range(zl))

    def step(s, _):
        @when(s < zl // 2)
        def _():
            loop(2, lambda k: product(2 * s + k))

        move(s, p, 1, rin, rs, rr)
        move(s, last - p, -1, lin, ls, lr)

        for delay, stage in ((0, stage1), (D2, stage2), (D3, stage3), (D4, stage4), (D5, stage5)):
            g = s - base - delay

            @when((g >= 0) & (g < groups))
            def _(g=g, stage=stage):
                stage(g)

        return 0

    lax.fori_loop(0, longest + groups + D5, step, 0)

    @when(jnp.logical_not(cross_src))
    def _():
        neighbour().wait_send()

    @when(sends_a)
    def _():
        for j in range(NX):
            leg_a(j).wait_send()

    @when(has_a)
    def _():
        leg_b().wait_send()

    def drain(d):
        whole = prod.at[d]

        @when(d > p)
        def _():
            send(whole, rin.at[d], rs.at[d], rr.at[d, 0], me).wait_send()

        @when(d < p)
        def _():
            send(whole, lin.at[d], ls.at[d], lr.at[d, 0], me).wait_send()

    loop(zl, drain)

    def drain_scan(g):
        all_of(g, a_s, a_r, lanes - 1).wait_send()
        all_of(g, b_s, b_r, lanes - 1).wait_send()
        for q in range(NY - 1):

            @when(y == q)
            def _(q=q):
                all_of(g, y_s, y_r, NY - 1 - q).wait_send()

        z_copy(g).wait_send()

    loop(groups, drain_scan)


def local(zl, tap_matrices, density_history, offsets, column_slots):
    m, c = tap_matrices.shape[1:]
    chunk = m // zl
    groups, rows, lanes = TICKS * HALVES, chunk // HALVES, 2 * NX
    piece, part = rows // lanes, c // (NX // 2)
    f32, bf16 = jnp.float32, jnp.bfloat16
    vmem, dma = pltpu.VMEM, pltpu.SemaphoreType.DMA
    out = pl.pallas_call(
        functools.partial(kernel, zl),
        out_shape=jax.ShapeDtypeStruct((TICKS, chunk, E), f32),
        in_specs=[
            pl.BlockSpec(memory_space=pltpu.SMEM),
            pl.BlockSpec(memory_space=pl.ANY),
            pl.BlockSpec(memory_space=pl.ANY),
            pl.BlockSpec(memory_space=pl.ANY),
        ],
        out_specs=pl.BlockSpec(memory_space=pltpu.VMEM),
        scratch_shapes=[
            vmem((1, E), jnp.int32),
            vmem((m, c), bf16),
            vmem((6, c, E), bf16),
            vmem((c, TICKS * E), bf16),
            vmem((zl, groups, rows, E), f32),
            vmem((zl, groups, rows, E), f32),
            vmem((zl, groups, rows, E), f32),
            vmem((groups, lanes, piece, E), f32),
            vmem((groups, lanes, piece, E), f32),
            vmem((groups, piece, E), f32),
            vmem((groups, NY, piece, E), f32),
            vmem((groups, piece, E), f32),
            vmem((groups, piece, E), f32),
            vmem((groups, piece, E), f32),
            vmem((groups, lanes, piece, E), f32),
            vmem((groups, rows, E), f32),
            vmem((part, E), bf16),
            dma((3,)),
            dma((1,)), dma((1,)),
            dma((NX,)), dma((1,)),
            dma((1,)), dma((NX,)),
            pltpu.SemaphoreType.REGULAR((2,)),
            dma((zl,)), dma((zl, groups)),
            dma((zl,)), dma((zl, groups)),
            dma((groups,)), dma((groups,)),
            dma((groups,)), dma((groups,)),
            dma((groups,)), dma((groups,)),
            dma((groups,)), dma((groups,)),
        ],
        compiler_params=pltpu.CompilerParams(collective_id=0, has_side_effects=True, vmem_limit_bytes=62 << 20),
    )(offsets, column_slots, tap_matrices.reshape(m, c), density_history)
    return out.transpose(1, 0, 2)[None]


def solution(mesh):
    return jax.shard_map(
        functools.partial(local, mesh.shape["col"]),
        mesh=mesh,
        in_specs=(P("lag", None, "col"), P("lag", "col", None), P("lag"), P("col", None)),
        out_specs=P("lag", "col", None, None),
        check_vma=False,
    )
```

```python
import functools

import jax
import jax.numpy as jnp
from jax import lax
from jax.experimental import pallas as pl
from jax.experimental.pallas import tpu as pltpu
from jax.sharding import PartitionSpec as P

MESH = pl.DeviceIdType.MESH
NX, NY = 4, 4
TICKS = 3
E = 128
HALVES = 2
HOP = 6
D2, D3, D4, D5 = 7, 14, 29, 36


def kernel(zl, off_ref, slots_hbm, tap_hbm, dens_hbm, out_ref, slots_ref, tap, win, dmat, prod, sent, sent_low, rin, rin_low, lin, lin_low, token, gath, pre, tot, yin, exb, zout, zin,
           fin, res, rela, loc, nb_s, nb_r, ca_s, ca_r, cb_s, cb_r, hello, rs, rr, ls, lr, a_s, a_r, y_s, y_r, z_s, z_r,
           b_s, b_r):
    lag, p = lax.axis_index("lag"), lax.axis_index("col")
    core = lag % 2
    x = (lag // 2) % NX
    zh = (lag // (2 * NX)) % 2
    y = lag // (4 * NX)
    lanes = 2 * NX
    lane = x * 2 + core
    groups = TICKS * HALVES
    rows = prod.shape[2]
    piece = rows // lanes
    part = win.shape[1] // (NX // 2)
    last = zl - 1

    def at(y_, zh_, x_, core_, p_):
        return (((y_ * 2 + zh_) * NX + x_) * 2 + core_, p_)

    def send(src, dst, ssem, rsem, to):
        return pltpu.make_async_remote_copy(src, dst, ssem, rsem, device_id=to, device_id_type=MESH)

    when = pl.when

    me = (lag, p)
    get_tap = pltpu.make_async_copy(tap_hbm, tap, loc.at[0])
    get_dens = pltpu.make_async_copy(dens_hbm, win.at[pl.ds(0, 4)], loc.at[1])
    get_slots = pltpu.make_async_copy(slots_hbm, slots_ref, loc.at[2])
    get_dens.start()
    get_tap.start()
    get_slots.start()
    z = zh * zl + p

    def round_z(q):
        q = (q + 2 * zl) % (2 * zl)
        return q // zl, q % zl

    cross_src = (x == 0) & (core == 0)
    cross_dst = (x == NX - 1) & (core == 1)
    final = lag == NY * 2 * lanes - 1
    sends_a = cross_src & (lag > 0)
    has_a = (core == 1) & ((y > 0) | (zh == 1))

    barrier = pltpu.get_barrier_semaphore()

    def greet(to):
        pl.semaphore_signal(barrier, inc=1, device_id=to, device_id_type=MESH)

    def loop(count, body):
        def one_more(j, _):
            body(j)
            return 0

        lax.fori_loop(0, count, one_more, 0)

    def others(body):
        loop(lanes - 1, lambda j: body((lane + 1 + j) % lanes))

    others(lambda j: greet(at(y, zh, j // 2, j % 2, p)))

    @when(p > 0)
    def _():
        greet((lag, p - 1))

    @when(p < last)
    def _():
        greet((lag, p + 1))

    loop(y, lambda j: greet(at(j, zh, x, core, p)))

    eighth, quarter = zl // 4, zl // 2

    def along(dz):
        zh_, p_ = round_z(z + dz)
        return at(y, zh_, x, core, p_)

    greet(along(eighth))
    greet(along(-eighth))

    @when(cross_dst & jnp.logical_not(final))
    def _():
        zh_, p_ = round_z(z - eighth)
        for j in range(NX):
            greet(at(y + zh, zh_, j, 1, p_))

    one = lambda c: c.astype(jnp.int32)
    far = round_z(z + eighth)[0]
    many = lanes - 1 + one(p > 0) + one(p < last) + NY - 1 - y + 2 + one((core == 1) & ((y > 0) | (far == 0)))
    pl.semaphore_wait(barrier, many)
    for dz in (eighth, -eighth):
        pl.semaphore_signal(hello.at[0], inc=1, device_id=along(dz), device_id_type=MESH)

    def vouch():
        pl.semaphore_wait(hello.at[0], 2)
        pl.semaphore_signal(hello.at[1], inc=1, device_id=along(-quarter), device_id_type=MESH)

    def vouched():
        pl.semaphore_wait(hello.at[1], 1)

    def neighbour():
        return send(dens_hbm.at[pl.ds(0, 2)], win.at[pl.ds(4, 2)], nb_s.at[0], nb_r.at[0], (lag - 1, p))

    @when(jnp.logical_not(cross_src))
    def _():
        neighbour().start()

    def part_of(ref, j, first):
        return ref.at[first + j // (NX // 2), pl.ds((j % (NX // 2)) * part, part)]

    def leg_a(j):
        return send(part_of(dens_hbm, j, 0), rela, ca_s.at[j], ca_r.at[0], at(y, zh, j, 1, p))

    def leg_b():
        return send(rela, part_of(win, x, 4), cb_s.at[0], cb_r.at[x], at(y - (1 - zh), 1 - zh, NX - 1, 1, p))

    @when(sends_a)
    def _():
        for j in range(NX):
            leg_a(j).start()

    @when(core == 1)
    def _():
        vouch()
        vouched()

    @when(has_a)
    def _():
        leg_a(0).wait_recv()
        leg_b().start()

    @when(final)
    def _():
        win[pl.ds(4, 2)] = jnp.zeros((2, *win.shape[1:]), win.dtype)

    get_dens.wait()

    @when(jnp.logical_not(cross_dst))
    def _():
        neighbour().wait_recv()

    @when(cross_dst & jnp.logical_not(final))
    def _():
        for j in range(NX):
            send(rela, part_of(win, j, 4), cb_s.at[0], cb_r.at[j], me).wait_recv()

    get_slots.wait()
    perm = (lax.broadcasted_iota(jnp.int32, (E, E), 0) == slots_ref[...]).astype(jnp.float32).astype(jnp.bfloat16)
    first = off_ref[0]
    for t in range(TICKS):
        dmat[:, t * E : (t + 1) * E] = jnp.dot(win[first + t], perm, preferred_element_type=jnp.float32).astype(jnp.bfloat16)
    get_tap.wait()
    chunk = rows * HALVES

    def product(k):
        d = jnp.where(k % 2 == 0, last - k // 2, k // 2)
        block = jnp.dot(tap[pl.ds(pl.multiple_of(d * chunk, chunk), chunk), :], dmat[...], preferred_element_type=jnp.float32)
        for t in range(TICKS):
            for h in range(HALVES):
                prod[d, t * HALVES + h] = block[h * rows : (h + 1) * rows, t * E : (t + 1) * E]

    @when(core == 0)
    def _():
        vouch()

    half = rows // 2

    def pack(value, d, g):
        high = value.astype(jnp.bfloat16)
        wide = high.astype(jnp.float32)
        share = (value - wide) / jnp.where(wide == 0.0, 1.0, wide) * 32768.0
        steps = (jnp.clip(share, -127.0, 127.0) + 128.5).astype(jnp.int32) - 128
        sent[d, g] = high
        sent_low[d, g] = (steps[:half] + steps[half:] * 256).astype(jnp.int16)

    def unpacked(high, low):
        both = low.astype(jnp.int32)
        upper = ((both + 128) & 255) - 128
        lower = (both - upper) >> 8
        wide = high.astype(jnp.float32)
        steps = jnp.concatenate([upper, lower], axis=0).astype(jnp.float32)
        return wide + wide * (steps * (1.0 / 32768.0))

    def move(step, hops, sign, buf, buf_low, ssem, rsem):
        def pass_on(d, g):
            send(sent.at[d, g], buf.at[d, g], ssem.at[d], rsem.at[d, g], (lag, p + sign)).start()
            send(sent_low.at[d, g], buf_low.at[d, g], ssem.at[d], rsem.at[d, g], (lag, p + sign)).start()

        @when((hops == 0) & (step < last))
        def _():
            d = last - step if sign > 0 else step

            def one_piece(g):
                pack(prod[d, g], d, g)
                pass_on(d, g)

            loop(groups, one_piece)

        n = step - HOP * hops

        @when((hops > 0) & (n >= 0) & (n < (zl - hops) * groups))
        def _():
            i = n // groups
            g = n % groups
            d = last - i if sign > 0 else i
            both = token.at[pl.ds(0, rows + half)]
            send(both, both, ssem.at[d], rsem.at[d, g], me).wait_recv()
            value = prod[d, g] + unpacked(buf[d, g], buf_low[d, g])

            @when(d == p)
            def _():
                prod[d, g] = value

            @when(d != p)
            def _():
                pack(value, d, g)
                pass_on(d, g)

    def mine(j):
        return pl.ds(pl.multiple_of(j * piece, piece), piece)

    def lane_at(j):
        return at(y, zh, j // 2, j % 2, p)

    def out_copy(g, j):
        return send(prod.at[p, g, mine(j)], gath.at[g, lane], a_s.at[g], a_r.at[g], lane_at(j))

    def back_copy(g, j):
        return send(fin.at[g, j], res.at[g, mine(lane)], b_s.at[g], b_r.at[g], lane_at(j))

    def y_copy(g, j):
        return send(tot.at[g], yin.at[g, y], y_s.at[g], y_r.at[g], at(j, zh, x, core, p))

    def z_copy(g):
        return send(zout.at[g], zin.at[g], z_s.at[g], z_r.at[g], at(y, 1 - zh, x, core, p))

    def all_of(g, sems, rsems, count):
        some = gath.at[g, pl.ds(0, count)]
        return send(some, some, sems.at[g], rsems.at[g], me)

    def stage1(g):
        gath[g, lane] = prod[p, g, mine(lane)]
        others(lambda j: out_copy(g, j).start())

    def stage2(g):
        all_of(g, a_s, a_r, lanes - 1).wait_recv()
        c = gath[g, 0]
        pre[g, 0] = c
        for j in range(1, lanes):
            c = c + gath[g, j]
            pre[g, j] = c
        tot[g] = c
        loop(NY - 1 - y, lambda j: y_copy(g, y + 1 + j).start())

    def stage3(g):
        exb[g] = jnp.zeros(exb.shape[1:], exb.dtype)
        for q in range(1, NY):

            @when(y == q)
            def _(q=q):
                all_of(g, y_s, y_r, q).wait_recv()

        def add(j):
            exb[g] = exb[g] + yin[g, j]

        loop(y, add)

        @when((core == 0) & (g == 0))
        def _():
            vouched()

        zout[g] = exb[g] + jnp.where(zh == 0, tot[g], 0.0)
        z_copy(g).start()

    def stage4(g):
        z_copy(g).wait_recv()
        e = exb[g] + zin[g]
        for j in range(lanes):
            fin[g, j] = pre[g, j] + e
        res[g, mine(lane)] = fin[g, lane]
        others(lambda j: back_copy(g, j).start())

    def stage5(g):
        all_of(g, b_s, b_r, lanes - 1).wait_recv()
        out_ref[g // HALVES, pl.ds(pl.multiple_of((g % HALVES) * rows, rows), rows)] = res[g]

    def ready(q):
        right = jnp.where(q > 0, HOP * q + (last - q) * groups, 0)
        left = jnp.where(q < last, HOP * (last - q) + q * groups, 0)
        return jnp.maximum(right, left)

    base = ready(p)
    longest = max(max(HOP * q + (last - q) * groups if q else 0, HOP * (last - q) + q * groups if q < last else 0) for q in range(zl))

    def step(s, _):
        @when(s < zl // 2)
        def _():
            loop(2, lambda k: product(2 * s + k))

        move(s, p, 1, rin, rin_low, rs, rr)
        move(s, last - p, -1, lin, lin_low, ls, lr)

        for delay, stage in ((0, stage1), (D2, stage2), (D3, stage3), (D4, stage4), (D5, stage5)):
            g = s - base - delay

            @when((g >= 0) & (g < groups))
            def _(g=g, stage=stage):
                stage(g)

        return 0

    lax.fori_loop(0, longest + groups + D5, step, 0)

    @when(jnp.logical_not(cross_src))
    def _():
        neighbour().wait_send()

    @when(sends_a)
    def _():
        for j in range(NX):
            leg_a(j).wait_send()

    @when(has_a)
    def _():
        leg_b().wait_send()

    def drain(d):
        @when(d > p)
        def _():
            send(token, token, rs.at[d], rr.at[d, 0], me).wait_send()

        @when(d < p)
        def _():
            send(token, token, ls.at[d], lr.at[d, 0], me).wait_send()

    loop(zl, drain)

    def drain_scan(g):
        all_of(g, a_s, a_r, lanes - 1).wait_send()
        all_of(g, b_s, b_r, lanes - 1).wait_send()
        for q in range(NY - 1):

            @when(y == q)
            def _(q=q):
                all_of(g, y_s, y_r, NY - 1 - q).wait_send()

        z_copy(g).wait_send()

    loop(groups, drain_scan)


def local(zl, tap_matrices, density_history, offsets, column_slots):
    m, c = tap_matrices.shape[1:]
    chunk = m // zl
    groups, rows, lanes = TICKS * HALVES, chunk // HALVES, 2 * NX
    piece, part = rows // lanes, c // (NX // 2)
    f32, bf16 = jnp.float32, jnp.bfloat16
    vmem, dma = pltpu.VMEM, pltpu.SemaphoreType.DMA
    out = pl.pallas_call(
        functools.partial(kernel, zl),
        out_shape=jax.ShapeDtypeStruct((TICKS, chunk, E), f32),
        in_specs=[
            pl.BlockSpec(memory_space=pltpu.SMEM),
            pl.BlockSpec(memory_space=pl.ANY),
            pl.BlockSpec(memory_space=pl.ANY),
            pl.BlockSpec(memory_space=pl.ANY),
        ],
        out_specs=pl.BlockSpec(memory_space=pltpu.VMEM),
        scratch_shapes=[
            vmem((1, E), jnp.int32),
            vmem((m, c), bf16),
            vmem((6, c, E), bf16),
            vmem((c, TICKS * E), bf16),
            vmem((zl, groups, rows, E), f32),
            vmem((zl, groups, rows, E), bf16), vmem((zl, groups, rows // 2, E), jnp.int16),
            vmem((zl, groups, rows, E), bf16), vmem((zl, groups, rows // 2, E), jnp.int16),
            vmem((zl, groups, rows, E), bf16), vmem((zl, groups, rows // 2, E), jnp.int16),
            vmem((groups * (rows + rows // 2), E), bf16),
            vmem((groups, lanes, piece, E), f32),
            vmem((groups, lanes, piece, E), f32),
            vmem((groups, piece, E), f32),
            vmem((groups, NY, piece, E), f32),
            vmem((groups, piece, E), f32),
            vmem((groups, piece, E), f32),
            vmem((groups, piece, E), f32),
            vmem((groups, lanes, piece, E), f32),
            vmem((groups, rows, E), f32),
            vmem((part, E), bf16),
            dma((3,)),
            dma((1,)), dma((1,)),
            dma((NX,)), dma((1,)),
            dma((1,)), dma((NX,)),
            pltpu.SemaphoreType.REGULAR((2,)),
            dma((zl,)), dma((zl, groups)),
            dma((zl,)), dma((zl, groups)),
            dma((groups,)), dma((groups,)),
            dma((groups,)), dma((groups,)),
            dma((groups,)), dma((groups,)),
            dma((groups,)), dma((groups,)),
        ],
        compiler_params=pltpu.CompilerParams(collective_id=0, has_side_effects=True, vmem_limit_bytes=62 << 20),
    )(offsets, column_slots, tap_matrices.reshape(m, c), density_history)
    return out.transpose(1, 0, 2)[None]


def solution(mesh):
    return jax.shard_map(
        functools.partial(local, mesh.shape["col"]),
        mesh=mesh,
        in_specs=(P("lag", None, "col"), P("lag", "col", None), P("lag"), P("col", None)),
        out_specs=P("lag", "col", None, None),
        check_vma=False,
    )
```

```python
import functools

import jax
import jax.numpy as jnp
from jax import lax
from jax.experimental import pallas as pl
from jax.experimental.pallas import tpu as pltpu
from jax.sharding import PartitionSpec as P

MESH = pl.DeviceIdType.MESH
NX, NY = 4, 4
TICKS = 3
E = 128
HALVES = 2
HOP, LATE_HOP = 8, 7
CUTS = 2
D2, D3, D4, D5 = 7, 14, 29, 36


def kernel(zl, off_ref, slots_hbm, tap_hbm, dens_hbm, out_ref, slots_ref, tap, win, dmat, prod, sent, sent_low, rin, rin_low, lin, lin_low, token, gath, pre, tot, yin, exb, zout, zin,
           fin, res, rela, loc, nb_s, nb_r, ca_s, ca_r, cb_s, cb_r, hello, rs, rr, ls, lr, a_s, a_r, y_s, y_r, z_s, z_r,
           b_s, b_r):
    lag, p = lax.axis_index("lag"), lax.axis_index("col")
    core = lag % 2
    x = (lag // 2) % NX
    zh = (lag // (2 * NX)) % 2
    y = lag // (4 * NX)
    lanes = 2 * NX
    lane = x * 2 + core
    groups = TICKS * HALVES
    rows = prod.shape[2]
    piece = rows // lanes
    part = win.shape[1] // (NX // 2)
    last = zl - 1

    def at(y_, zh_, x_, core_, p_):
        return (((y_ * 2 + zh_) * NX + x_) * 2 + core_, p_)

    def send(src, dst, ssem, rsem, to):
        return pltpu.make_async_remote_copy(src, dst, ssem, rsem, device_id=to, device_id_type=MESH)

    when = pl.when

    me = (lag, p)
    get_tap = pltpu.make_async_copy(tap_hbm, tap, loc.at[0])
    get_dens = pltpu.make_async_copy(dens_hbm, win.at[pl.ds(0, 4)], loc.at[1])
    get_slots = pltpu.make_async_copy(slots_hbm, slots_ref, loc.at[2])
    get_dens.start()
    get_tap.start()
    get_slots.start()
    z = zh * zl + p

    def round_z(q):
        q = (q + 2 * zl) % (2 * zl)
        return q // zl, q % zl

    cross_src = (x == 0) & (core == 0)
    cross_dst = (x == NX - 1) & (core == 1)
    final = lag == NY * 2 * lanes - 1
    sends_a = cross_src & (lag > 0)
    has_a = (core == 1) & ((y > 0) | (zh == 1))

    barrier = pltpu.get_barrier_semaphore()

    def greet(to):
        pl.semaphore_signal(barrier, inc=1, device_id=to, device_id_type=MESH)

    def loop(count, body):
        def one_more(j, _):
            body(j)
            return 0

        lax.fori_loop(0, count, one_more, 0)

    def others(body):
        loop(lanes - 1, lambda j: body((lane + 1 + j) % lanes))

    others(lambda j: greet(at(y, zh, j // 2, j % 2, p)))

    @when(p > 0)
    def _():
        greet((lag, p - 1))

    @when(p < last)
    def _():
        greet((lag, p + 1))

    loop(y, lambda j: greet(at(j, zh, x, core, p)))

    eighth, quarter = zl // 4, zl // 2

    def along(dz):
        zh_, p_ = round_z(z + dz)
        return at(y, zh_, x, core, p_)

    greet(along(eighth))
    greet(along(-eighth))

    @when(cross_dst & jnp.logical_not(final))
    def _():
        for j in range(NX):
            greet(at(y + zh, 1 - zh, j, 1, p))

    one = lambda c: c.astype(jnp.int32)
    many = lanes - 1 + one(p > 0) + one(p < last) + NY - 1 - y + 2 + one(has_a)
    pl.semaphore_wait(barrier, many)
    for dz in (eighth, -eighth):
        pl.semaphore_signal(hello.at[0], inc=1, device_id=along(dz), device_id_type=MESH)

    def vouch():
        pl.semaphore_wait(hello.at[0], 2)
        pl.semaphore_signal(hello.at[1], inc=1, device_id=along(-quarter), device_id_type=MESH)

    def vouched():
        pl.semaphore_wait(hello.at[1], 1)

    def neighbour():
        return send(dens_hbm.at[pl.ds(0, 2)], win.at[pl.ds(4, 2)], nb_s.at[0], nb_r.at[0], (lag - 1, p))

    @when(jnp.logical_not(cross_src))
    def _():
        neighbour().start()

    piece_of = part // CUTS

    def part_of(ref, j, first, i=0, size=part):
        return ref.at[first + j // (NX // 2), pl.ds((j % (NX // 2)) * part + i * piece_of, size)]

    def leg_a(j, i):
        return send(part_of(dens_hbm, j, 0, i, piece_of), rela.at[i], ca_s.at[j], ca_r.at[i], at(y, zh, j, 1, p))

    def leg_b(i):
        there = at(y - (1 - zh), 1 - zh, NX - 1, 1, p)
        return send(rela.at[i], part_of(win, x, 4, i, piece_of), cb_s.at[i], cb_r.at[x], there)

    @when(sends_a)
    def _():
        for i in range(CUTS):
            for j in range(NX):
                leg_a(j, i).start()

    @when(has_a)
    def _():
        for i in range(CUTS):
            leg_a(0, i).wait_recv()
            leg_b(i).start()

    @when(final)
    def _():
        win[pl.ds(4, 2)] = jnp.zeros((2, *win.shape[1:]), win.dtype)

    get_dens.wait()

    @when(jnp.logical_not(cross_dst))
    def _():
        neighbour().wait_recv()

    @when(cross_dst & jnp.logical_not(final))
    def _():
        for j in range(NX):
            send(part_of(win, j, 4), part_of(win, j, 4), cb_s.at[0], cb_r.at[j], me).wait_recv()

    get_slots.wait()
    perm = (lax.broadcasted_iota(jnp.int32, (E, E), 0) == slots_ref[...]).astype(jnp.float32).astype(jnp.bfloat16)
    first = off_ref[0]
    for t in range(TICKS):
        dmat[:, t * E : (t + 1) * E] = jnp.dot(win[first + t], perm, preferred_element_type=jnp.float32).astype(jnp.bfloat16)
    get_tap.wait()
    chunk = rows * HALVES

    def product(k):
        d = jnp.where(k % 2 == 0, last - k // 2, k // 2)
        block = jnp.dot(tap[pl.ds(pl.multiple_of(d * chunk, chunk), chunk), :], dmat[...], preferred_element_type=jnp.float32)
        for t in range(TICKS):
            for h in range(HALVES):
                prod[d, t * HALVES + h] = block[h * rows : (h + 1) * rows, t * E : (t + 1) * E]

    vouch()

    half = rows // 2
    hop = jnp.where(cross_dst, LATE_HOP, HOP)

    def pack(value, d, g):
        high = value.astype(jnp.bfloat16)
        wide = high.astype(jnp.float32)
        share = (value - wide) / jnp.where(wide == 0.0, 1.0, wide) * 32768.0
        steps = (jnp.clip(share, -127.0, 127.0) + 128.5).astype(jnp.int32) - 128
        sent[d, g] = high
        sent_low[d, g] = (steps[:half] + steps[half:] * 256).astype(jnp.int16)

    def unpacked(high, low):
        both = low.astype(jnp.int32)
        upper = ((both + 128) & 255) - 128
        lower = (both - upper) >> 8
        wide = high.astype(jnp.float32)
        steps = jnp.concatenate([upper, lower], axis=0).astype(jnp.float32)
        return wide + wide * (steps * (1.0 / 32768.0))

    def move(step, hops, sign, buf, buf_low, ssem, rsem):
        def pass_on(d, g):
            send(sent.at[d, g], buf.at[d, g], ssem.at[d], rsem.at[d, g], (lag, p + sign)).start()
            send(sent_low.at[d, g], buf_low.at[d, g], ssem.at[d], rsem.at[d, g], (lag, p + sign)).start()

        @when((hops == 0) & (step < last))
        def _():
            d = last - step if sign > 0 else step

            def one_piece(g):
                pack(prod[d, g], d, g)
                pass_on(d, g)

            loop(groups, one_piece)

        n = step - hop * hops

        @when((hops > 0) & (n >= 0) & (n < (zl - hops) * groups))
        def _():
            i = n // groups
            g = n % groups
            d = last - i if sign > 0 else i
            both = token.at[pl.ds(0, rows + half)]
            send(both, both, ssem.at[d], rsem.at[d, g], me).wait_recv()
            value = prod[d, g] + unpacked(buf[d, g], buf_low[d, g])

            @when(d == p)
            def _():
                prod[d, g] = value

            @when(d != p)
            def _():
                pack(value, d, g)
                pass_on(d, g)

    def mine(j):
        return pl.ds(pl.multiple_of(j * piece, piece), piece)

    def lane_at(j):
        return at(y, zh, j // 2, j % 2, p)

    def out_copy(g, j):
        return send(prod.at[p, g, mine(j)], gath.at[g, lane], a_s.at[g], a_r.at[g], lane_at(j))

    def back_copy(g, j):
        return send(fin.at[g, j], res.at[g, mine(lane)], b_s.at[g], b_r.at[g], lane_at(j))

    def y_copy(g, j):
        return send(tot.at[g], yin.at[g, y], y_s.at[g], y_r.at[g], at(j, zh, x, core, p))

    def z_copy(g):
        return send(zout.at[g], zin.at[g], z_s.at[g], z_r.at[g], at(y, 1 - zh, x, core, p))

    def all_of(g, sems, rsems, count):
        some = gath.at[g, pl.ds(0, count)]
        return send(some, some, sems.at[g], rsems.at[g], me)

    def stage1(g):
        gath[g, lane] = prod[p, g, mine(lane)]
        others(lambda j: out_copy(g, j).start())

    def stage2(g):
        all_of(g, a_s, a_r, lanes - 1).wait_recv()
        c = gath[g, 0]
        pre[g, 0] = c
        for j in range(1, lanes):
            c = c + gath[g, j]
            pre[g, j] = c
        tot[g] = c
        loop(NY - 1 - y, lambda j: y_copy(g, y + 1 + j).start())

    def stage3(g):
        exb[g] = jnp.zeros(exb.shape[1:], exb.dtype)
        for q in range(1, NY):

            @when(y == q)
            def _(q=q):
                all_of(g, y_s, y_r, q).wait_recv()

        def add(j):
            exb[g] = exb[g] + yin[g, j]

        loop(y, add)

        @when(g == 0)
        def _():
            vouched()

        zout[g] = exb[g] + jnp.where(zh == 0, tot[g], 0.0)
        z_copy(g).start()

    def stage4(g):
        z_copy(g).wait_recv()
        e = exb[g] + zin[g]
        for j in range(lanes):
            fin[g, j] = pre[g, j] + e
        res[g, mine(lane)] = fin[g, lane]
        others(lambda j: back_copy(g, j).start())

    def stage5(g):
        all_of(g, b_s, b_r, lanes - 1).wait_recv()
        out_ref[g // HALVES, pl.ds(pl.multiple_of((g % HALVES) * rows, rows), rows)] = res[g]

    def ready(q):
        right = jnp.where(q > 0, hop * q + (last - q) * groups, 0)
        left = jnp.where(q < last, hop * (last - q) + q * groups, 0)
        return jnp.maximum(right, left)

    base = ready(p)
    most = max(HOP, LATE_HOP)
    longest = max(most * q + max(last - q, 0) * groups for q in range(zl))

    def step(s, _):
        @when(s < zl // 2)
        def _():
            loop(2, lambda k: product(2 * s + k))

        move(s, p, 1, rin, rin_low, rs, rr)
        move(s, last - p, -1, lin, lin_low, ls, lr)

        for delay, stage in ((0, stage1), (D2, stage2), (D3, stage3), (D4, stage4), (D5, stage5)):
            g = s - base - delay

            @when((g >= 0) & (g < groups))
            def _(g=g, stage=stage):
                stage(g)

        return 0

    lax.fori_loop(0, longest + groups + D5, step, 0)

    @when(jnp.logical_not(cross_src))
    def _():
        neighbour().wait_send()

    @when(sends_a)
    def _():
        for j in range(NX):
            send(part_of(dens_hbm, j, 0), part_of(win, j, 4), ca_s.at[j], ca_r.at[0], me).wait_send()

    @when(has_a)
    def _():
        for i in range(CUTS):
            leg_b(i).wait_send()

    def drain(d):
        @when(d > p)
        def _():
            send(token, token, rs.at[d], rr.at[d, 0], me).wait_send()

        @when(d < p)
        def _():
            send(token, token, ls.at[d], lr.at[d, 0], me).wait_send()

    loop(zl, drain)

    def drain_scan(g):
        all_of(g, a_s, a_r, lanes - 1).wait_send()
        all_of(g, b_s, b_r, lanes - 1).wait_send()
        for q in range(NY - 1):

            @when(y == q)
            def _(q=q):
                all_of(g, y_s, y_r, NY - 1 - q).wait_send()

        z_copy(g).wait_send()

    loop(groups, drain_scan)


def local(zl, tap_matrices, density_history, offsets, column_slots):
    m, c = tap_matrices.shape[1:]
    chunk = m // zl
    groups, rows, lanes = TICKS * HALVES, chunk // HALVES, 2 * NX
    piece, part = rows // lanes, c // (NX // 2)
    f32, bf16 = jnp.float32, jnp.bfloat16
    vmem, dma = pltpu.VMEM, pltpu.SemaphoreType.DMA
    out = pl.pallas_call(
        functools.partial(kernel, zl),
        out_shape=jax.ShapeDtypeStruct((TICKS, chunk, E), f32),
        in_specs=[
            pl.BlockSpec(memory_space=pltpu.SMEM),
            pl.BlockSpec(memory_space=pl.ANY),
            pl.BlockSpec(memory_space=pl.ANY),
            pl.BlockSpec(memory_space=pl.ANY),
        ],
        out_specs=pl.BlockSpec(memory_space=pltpu.VMEM),
        scratch_shapes=[
            vmem((1, E), jnp.int32),
            vmem((m, c), bf16),
            vmem((6, c, E), bf16),
            vmem((c, TICKS * E), bf16),
            vmem((zl, groups, rows, E), f32),
            vmem((zl, groups, rows, E), bf16), vmem((zl, groups, rows // 2, E), jnp.int16),
            vmem((zl, groups, rows, E), bf16), vmem((zl, groups, rows // 2, E), jnp.int16),
            vmem((zl, groups, rows, E), bf16), vmem((zl, groups, rows // 2, E), jnp.int16),
            vmem((groups * (rows + rows // 2), E), bf16),
            vmem((groups, lanes, piece, E), f32),
            vmem((groups, lanes, piece, E), f32),
            vmem((groups, piece, E), f32),
            vmem((groups, NY, piece, E), f32),
            vmem((groups, piece, E), f32),
            vmem((groups, piece, E), f32),
            vmem((groups, piece, E), f32),
            vmem((groups, lanes, piece, E), f32),
            vmem((groups, rows, E), f32),
            vmem((CUTS, part // CUTS, E), bf16),
            dma((3,)),
            dma((1,)), dma((1,)),
            dma((NX,)), dma((CUTS,)),
            dma((CUTS,)), dma((NX,)),
            pltpu.SemaphoreType.REGULAR((2,)),
            dma((zl,)), dma((zl, groups)),
            dma((zl,)), dma((zl, groups)),
            dma((groups,)), dma((groups,)),
            dma((groups,)), dma((groups,)),
            dma((groups,)), dma((groups,)),
            dma((groups,)), dma((groups,)),
        ],
        compiler_params=pltpu.CompilerParams(collective_id=0, has_side_effects=True, vmem_limit_bytes=62 << 20),
    )(offsets, column_slots, tap_matrices.reshape(m, c), density_history)
    return out.transpose(1, 0, 2)[None]


def solution(mesh):
    return jax.shard_map(
        functools.partial(local, mesh.shape["col"]),
        mesh=mesh,
        in_specs=(P("lag", None, "col"), P("lag", "col", None), P("lag"), P("col", None)),
        out_specs=P("lag", "col", None, None),
        check_vma=False,
    )
```

```python
import functools

import jax
import jax.numpy as jnp
from jax import lax
from jax.experimental import pallas as pl
from jax.experimental.pallas import tpu as pltpu
from jax.sharding import PartitionSpec as P

MESH = pl.DeviceIdType.MESH
NX, NY = 4, 4
TICKS = 3
E = 128
HALVES = 2
HOP, LATE_HOP = 8, 7
VOUCH = 7
CUTS = 2
D2, D3, D4, D5 = 7, 14, 29, 36


def kernel(zl, off_ref, slots_hbm, tap_hbm, dens_hbm, out_ref, slots_ref, tap, win, dmat, prod, sent, sent_low, rin, rin_low, lin, lin_low, token, gath, pre, tot, yin, exb, zout, zin,
           fin, res, rela, loc, nb_s, nb_r, ca_s, ca_r, cb_s, cb_r, hello, rs, rr, ls, lr, a_s, a_r, y_s, y_r, z_s, z_r,
           b_s, b_r):
    lag, p = lax.axis_index("lag"), lax.axis_index("col")
    core = lag % 2
    x = (lag // 2) % NX
    zh = (lag // (2 * NX)) % 2
    y = lag // (4 * NX)
    lanes = 2 * NX
    lane = x * 2 + core
    groups = TICKS * HALVES
    rows = prod.shape[2]
    piece = rows // lanes
    part = win.shape[1] // (NX // 2)
    last = zl - 1

    def at(y_, zh_, x_, core_, p_):
        return (((y_ * 2 + zh_) * NX + x_) * 2 + core_, p_)

    def send(src, dst, ssem, rsem, to):
        return pltpu.make_async_remote_copy(src, dst, ssem, rsem, device_id=to, device_id_type=MESH)

    when = pl.when

    me = (lag, p)
    get_tap = pltpu.make_async_copy(tap_hbm, tap, loc.at[0])
    get_dens = pltpu.make_async_copy(dens_hbm, win.at[pl.ds(0, 4)], loc.at[1])
    get_slots = pltpu.make_async_copy(slots_hbm, slots_ref, loc.at[2])
    get_dens.start()
    get_tap.start()
    get_slots.start()
    z = zh * zl + p

    def round_z(q):
        q = (q + 2 * zl) % (2 * zl)
        return q // zl, q % zl

    cross_src = (x == 0) & (core == 0)
    cross_dst = (x == NX - 1) & (core == 1)
    final = lag == NY * 2 * lanes - 1
    sends_a = cross_src & (lag > 0)
    has_a = (core == 1) & ((y > 0) | (zh == 1))

    barrier = pltpu.get_barrier_semaphore()

    def greet(to):
        pl.semaphore_signal(barrier, inc=1, device_id=to, device_id_type=MESH)

    def loop(count, body):
        def one_more(j, _):
            body(j)
            return 0

        lax.fori_loop(0, count, one_more, 0)

    def others(body):
        loop(lanes - 1, lambda j: body((lane + 1 + j) % lanes))

    others(lambda j: greet(at(y, zh, j // 2, j % 2, p)))

    @when(p > 0)
    def _():
        greet((lag, p - 1))

    @when(p < last)
    def _():
        greet((lag, p + 1))

    loop(y, lambda j: greet(at(j, zh, x, core, p)))

    eighth, quarter = zl // 4, zl // 2

    def along(dz):
        zh_, p_ = round_z(z + dz)
        return at(y, zh_, x, core, p_)

    greet(along(eighth))
    greet(along(-eighth))

    @when(cross_dst & jnp.logical_not(final))
    def _():
        for j in range(NX):
            greet(at(y + zh, 1 - zh, j, 1, p))

    one = lambda c: c.astype(jnp.int32)
    many = lanes - 1 + one(p > 0) + one(p < last) + NY - 1 - y + 2 + one(has_a)
    pl.semaphore_wait(barrier, many)
    for dz in (eighth, -eighth):
        pl.semaphore_signal(hello.at[0], inc=1, device_id=along(dz), device_id_type=MESH)

    def vouch():
        pl.semaphore_wait(hello.at[0], 2)
        pl.semaphore_signal(hello.at[1], inc=1, device_id=along(-quarter), device_id_type=MESH)

    def vouched():
        pl.semaphore_wait(hello.at[1], 1)

    def neighbour():
        return send(dens_hbm.at[pl.ds(0, 2)], win.at[pl.ds(4, 2)], nb_s.at[0], nb_r.at[0], (lag - 1, p))

    @when(jnp.logical_not(cross_src))
    def _():
        neighbour().start()

    piece_of = part // CUTS

    def part_of(ref, j, first, i=0, size=part):
        return ref.at[first + j // (NX // 2), pl.ds((j % (NX // 2)) * part + i * piece_of, size)]

    def leg_a(j, i):
        return send(part_of(dens_hbm, j, 0, i, piece_of), rela.at[i], ca_s.at[j], ca_r.at[i], at(y, zh, j, 1, p))

    def leg_b(i):
        there = at(y - (1 - zh), 1 - zh, NX - 1, 1, p)
        return send(rela.at[i], part_of(win, x, 4, i, piece_of), cb_s.at[i], cb_r.at[x], there)

    @when(sends_a)
    def _():
        for i in range(CUTS):
            for j in range(NX):
                leg_a(j, i).start()

    @when(has_a)
    def _():
        for i in range(CUTS):
            leg_a(0, i).wait_recv()
            leg_b(i).start()

    @when(final)
    def _():
        win[pl.ds(4, 2)] = jnp.zeros((2, *win.shape[1:]), win.dtype)

    get_dens.wait()

    @when(jnp.logical_not(cross_dst))
    def _():
        neighbour().wait_recv()

    @when(cross_dst & jnp.logical_not(final))
    def _():
        for j in range(NX):
            send(part_of(win, j, 4), part_of(win, j, 4), cb_s.at[0], cb_r.at[j], me).wait_recv()

    get_slots.wait()
    perm = (lax.broadcasted_iota(jnp.int32, (E, E), 0) == slots_ref[...]).astype(jnp.float32).astype(jnp.bfloat16)
    first = off_ref[0]
    for t in range(TICKS):
        dmat[:, t * E : (t + 1) * E] = jnp.dot(win[first + t], perm, preferred_element_type=jnp.float32).astype(jnp.bfloat16)
    get_tap.wait()
    chunk = rows * HALVES

    def product(k):
        d = jnp.where(k % 2 == 0, last - k // 2, k // 2)
        block = jnp.dot(tap[pl.ds(pl.multiple_of(d * chunk, chunk), chunk), :], dmat[...], preferred_element_type=jnp.float32)
        for t in range(TICKS):
            for h in range(HALVES):
                prod[d, t * HALVES + h] = block[h * rows : (h + 1) * rows, t * E : (t + 1) * E]


    half = rows // 2
    hop = jnp.where(cross_dst, LATE_HOP, HOP)

    def pack(value, d, g):
        high = value.astype(jnp.bfloat16)
        wide = high.astype(jnp.float32)
        share = (value - wide) / jnp.where(wide == 0.0, 1.0, wide) * 32768.0
        steps = (jnp.clip(share, -127.0, 127.0) + 128.5).astype(jnp.int32) - 128
        sent[d, g] = high
        sent_low[d, g] = (steps[:half] + steps[half:] * 256).astype(jnp.int16)

    def unpacked(high, low):
        both = low.astype(jnp.int32)
        upper = ((both + 128) & 255) - 128
        lower = (both - upper) >> 8
        wide = high.astype(jnp.float32)
        steps = jnp.concatenate([upper, lower], axis=0).astype(jnp.float32)
        return wide + wide * (steps * (1.0 / 32768.0))

    def move(step, hops, sign, buf, buf_low, ssem, rsem):
        def pass_on(d, g):
            send(sent.at[d, g], buf.at[d, g], ssem.at[d], rsem.at[d, g], (lag, p + sign)).start()
            send(sent_low.at[d, g], buf_low.at[d, g], ssem.at[d], rsem.at[d, g], (lag, p + sign)).start()

        @when((hops == 0) & (step < last))
        def _():
            d = last - step if sign > 0 else step

            def one_piece(g):
                pack(prod[d, g], d, g)
                pass_on(d, g)

            loop(groups, one_piece)

        n = step - hop * hops

        @when((hops > 0) & (n >= 0) & (n < (zl - hops) * groups))
        def _():
            i = n // groups
            g = n % groups
            d = last - i if sign > 0 else i
            both = token.at[pl.ds(0, rows + half)]
            send(both, both, ssem.at[d], rsem.at[d, g], me).wait_recv()
            value = prod[d, g] + unpacked(buf[d, g], buf_low[d, g])

            @when(d == p)
            def _():
                prod[d, g] = value

            @when(d != p)
            def _():
                pack(value, d, g)
                pass_on(d, g)

    def mine(j):
        return pl.ds(pl.multiple_of(j * piece, piece), piece)

    def lane_at(j):
        return at(y, zh, j // 2, j % 2, p)

    def out_copy(g, j):
        return send(prod.at[p, g, mine(j)], gath.at[g, lane], a_s.at[g], a_r.at[g], lane_at(j))

    def back_copy(g, j):
        return send(fin.at[g, j], res.at[g, mine(lane)], b_s.at[g], b_r.at[g], lane_at(j))

    def y_copy(g, j):
        return send(tot.at[g], yin.at[g, y], y_s.at[g], y_r.at[g], at(j, zh, x, core, p))

    def z_copy(g):
        return send(zout.at[g], zin.at[g], z_s.at[g], z_r.at[g], at(y, 1 - zh, x, core, p))

    def all_of(g, sems, rsems, count):
        some = gath.at[g, pl.ds(0, count)]
        return send(some, some, sems.at[g], rsems.at[g], me)

    def stage1(g):
        gath[g, lane] = prod[p, g, mine(lane)]
        others(lambda j: out_copy(g, j).start())

    def stage2(g):
        all_of(g, a_s, a_r, lanes - 1).wait_recv()
        c = gath[g, 0]
        pre[g, 0] = c
        for j in range(1, lanes):
            c = c + gath[g, j]
            pre[g, j] = c
        tot[g] = c
        loop(NY - 1 - y, lambda j: y_copy(g, y + 1 + j).start())

    def stage3(g):
        exb[g] = jnp.zeros(exb.shape[1:], exb.dtype)
        for q in range(1, NY):

            @when(y == q)
            def _(q=q):
                all_of(g, y_s, y_r, q).wait_recv()

        def add(j):
            exb[g] = exb[g] + yin[g, j]

        loop(y, add)

        @when(g == 0)
        def _():
            vouched()

        zout[g] = exb[g] + jnp.where(zh == 0, tot[g], 0.0)
        z_copy(g).start()

    def stage4(g):
        z_copy(g).wait_recv()
        e = exb[g] + zin[g]
        for j in range(lanes):
            fin[g, j] = pre[g, j] + e
        res[g, mine(lane)] = fin[g, lane]
        others(lambda j: back_copy(g, j).start())

    def stage5(g):
        all_of(g, b_s, b_r, lanes - 1).wait_recv()
        out_ref[g // HALVES, pl.ds(pl.multiple_of((g % HALVES) * rows, rows), rows)] = res[g]

    def ready(q):
        right = jnp.where(q > 0, hop * q + (last - q) * groups, 0)
        left = jnp.where(q < last, hop * (last - q) + q * groups, 0)
        return jnp.maximum(right, left)

    base = ready(p)
    most = max(HOP, LATE_HOP)
    longest = max(most * q + max(last - q, 0) * groups for q in range(zl))

    def step(s, _):
        @when(s < zl // 2)
        def _():
            loop(2, lambda k: product(2 * s + k))

        pl.when(s == VOUCH)(vouch)
        move(s, p, 1, rin, rin_low, rs, rr)
        move(s, last - p, -1, lin, lin_low, ls, lr)

        for delay, stage in ((0, stage1), (D2, stage2), (D3, stage3), (D4, stage4), (D5, stage5)):
            g = s - base - delay

            @when((g >= 0) & (g < groups))
            def _(g=g, stage=stage):
                stage(g)

        return 0

    lax.fori_loop(0, longest + groups + D5, step, 0)

    @when(jnp.logical_not(cross_src))
    def _():
        neighbour().wait_send()

    @when(sends_a)
    def _():
        for j in range(NX):
            send(part_of(dens_hbm, j, 0), part_of(win, j, 4), ca_s.at[j], ca_r.at[0], me).wait_send()

    @when(has_a)
    def _():
        for i in range(CUTS):
            leg_b(i).wait_send()

    def drain(d):
        @when(d > p)
        def _():
            send(token, token, rs.at[d], rr.at[d, 0], me).wait_send()

        @when(d < p)
        def _():
            send(token, token, ls.at[d], lr.at[d, 0], me).wait_send()

    loop(zl, drain)

    def drain_scan(g):
        all_of(g, a_s, a_r, lanes - 1).wait_send()
        all_of(g, b_s, b_r, lanes - 1).wait_send()
        for q in range(NY - 1):

            @when(y == q)
            def _(q=q):
                all_of(g, y_s, y_r, NY - 1 - q).wait_send()

        z_copy(g).wait_send()

    loop(groups, drain_scan)


def local(zl, tap_matrices, density_history, offsets, column_slots):
    m, c = tap_matrices.shape[1:]
    chunk = m // zl
    groups, rows, lanes = TICKS * HALVES, chunk // HALVES, 2 * NX
    piece, part = rows // lanes, c // (NX // 2)
    f32, bf16 = jnp.float32, jnp.bfloat16
    vmem, dma = pltpu.VMEM, pltpu.SemaphoreType.DMA
    out = pl.pallas_call(
        functools.partial(kernel, zl),
        out_shape=jax.ShapeDtypeStruct((TICKS, chunk, E), f32),
        in_specs=[
            pl.BlockSpec(memory_space=pltpu.SMEM),
            pl.BlockSpec(memory_space=pl.ANY),
            pl.BlockSpec(memory_space=pl.ANY),
            pl.BlockSpec(memory_space=pl.ANY),
        ],
        out_specs=pl.BlockSpec(memory_space=pltpu.VMEM),
        scratch_shapes=[
            vmem((1, E), jnp.int32),
            vmem((m, c), bf16),
            vmem((6, c, E), bf16),
            vmem((c, TICKS * E), bf16),
            vmem((zl, groups, rows, E), f32),
            vmem((zl, groups, rows, E), bf16), vmem((zl, groups, rows // 2, E), jnp.int16),
            vmem((zl, groups, rows, E), bf16), vmem((zl, groups, rows // 2, E), jnp.int16),
            vmem((zl, groups, rows, E), bf16), vmem((zl, groups, rows // 2, E), jnp.int16),
            vmem((groups * (rows + rows // 2), E), bf16),
            vmem((groups, lanes, piece, E), f32),
            vmem((groups, lanes, piece, E), f32),
            vmem((groups, piece, E), f32),
            vmem((groups, NY, piece, E), f32),
            vmem((groups, piece, E), f32),
            vmem((groups, piece, E), f32),
            vmem((groups, piece, E), f32),
            vmem((groups, lanes, piece, E), f32),
            vmem((groups, rows, E), f32),
            vmem((CUTS, part // CUTS, E), bf16),
            dma((3,)),
            dma((1,)), dma((1,)),
            dma((NX,)), dma((CUTS,)),
            dma((CUTS,)), dma((NX,)),
            pltpu.SemaphoreType.REGULAR((2,)),
            dma((zl,)), dma((zl, groups)),
            dma((zl,)), dma((zl, groups)),
            dma((groups,)), dma((groups,)),
            dma((groups,)), dma((groups,)),
            dma((groups,)), dma((groups,)),
            dma((groups,)), dma((groups,)),
        ],
        compiler_params=pltpu.CompilerParams(collective_id=0, has_side_effects=True, vmem_limit_bytes=62 << 20),
    )(offsets, column_slots, tap_matrices.reshape(m, c), density_history)
    return out.transpose(1, 0, 2)[None]


def solution(mesh):
    return jax.shard_map(
        functools.partial(local, mesh.shape["col"]),
        mesh=mesh,
        in_specs=(P("lag", None, "col"), P("lag", "col", None), P("lag"), P("col", None)),
        out_specs=P("lag", "col", None, None),
        check_vma=False,
    )
```
